32 devices in a mesh: tensor: 4 (over z), dp: 4 (over y, x), ctx: 2 (over core).
Axes of the slice: x: 2, y: 2, z: 4, core: 2. Of those that a mesh axis runs over, the one named last changes fastest.
Arguments:
- tokens: bfloat16 [1024, 2048], P(('dp', 'ctx')), may hold values from -6 to 6
- cotangent: bfloat16 [1024, 2048], P(('dp', 'ctx')), may hold values from -6 to 6
- sequence_loops: int32 [4], P('dp'), may hold values from 0 to 1
- attention_gain: bfloat16 [2048], P(('dp', 'ctx')), may hold values from 0.099609375 to 1.8984375
- query_weight: bfloat16 [2048, 2048], P(('dp', 'ctx'), 'tensor'), may hold values from -0.125 to 0.125
- key_weight: bfloat16 [2048, 256], P(('dp', 'ctx')), may hold values from -0.125 to 0.125
- value_weight: bfloat16 [2048, 256], P(('dp', 'ctx')), may hold values from -0.125 to 0.125
- attention_output_weight: bfloat16 [2048, 2048], P('tensor', ('dp', 'ctx')), may hold values from -2 to 2
- lowrank_output_first: bfloat16 [2, 2048, 256], P(None, ('tensor', 'dp', 'ctx')), may hold values from -1.5 to 1.5
- lowrank_output_second: bfloat16 [2, 256, 2048], P(None, None, ('dp', 'ctx')), may hold values from -0.375 to 0.375
- feedforward_gain: bfloat16 [2048], P(('dp', 'ctx')), may hold values from 0.099609375 to 1.8984375
- gate_weight: bfloat16 [2048, 16384], P(('dp', 'ctx'), 'tensor'), may hold values from -0.125 to 0.125
- up_weight: bfloat16 [2048, 16384], P(('dp', 'ctx'), 'tensor'), may hold values from -0.125 to 0.125
- down_weight: bfloat16 [16384, 2048], P('tensor', ('dp', 'ctx')), may hold values from -0.046875 to 0.046875
- lowrank_down_first: bfloat16 [2, 16384, 256], P(None, ('tensor', 'dp', 'ctx')), may hold values from -0.046875 to 0.046875
- lowrank_down_second: bfloat16 [2, 256, 2048], P(None, None, ('dp', 'ctx')), may hold values from -0.375 to 0.375
Outputs:
- out: bfloat16 [1024, 2048], P(('dp', 'ctx'))
- input_grad: bfloat16 [1024, 2048], P(('dp', 'ctx'))
- grad_attn_gain: float32 [2048], P(('dp', 'ctx'))
- grad_w_query: float32 [2048, 2048], P(('dp', 'ctx'), 'tensor')
- grad_w_key: float32 [2048, 256], P(('dp', 'ctx'))
- grad_w_value: float32 [2048, 256], P(('dp', 'ctx'))
- grad_w_out: float32 [2048, 2048], P('tensor', ('dp', 'ctx'))
- grad_lora_out_a: float32 [2, 2048, 256], P(None, ('tensor', 'dp', 'ctx'))
- grad_lora_out_b: float32 [2, 256, 2048], P(None, None, ('dp', 'ctx'))
- grad_mlp_gain: float32 [2048], P(('dp', 'ctx'))
- grad_w_gate: float32 [2048, 16384], P(('dp', 'ctx'), 'tensor')
- grad_w_up: float32 [2048, 16384], P(('dp', 'ctx'), 'tensor')
- grad_w_down: float32 [16384, 2048], P('tensor', ('dp', 'ctx'))
- grad_lora_down_a: float32 [2, 16384, 256], P(None, ('tensor', 'dp', 'ctx'))
- grad_lora_down_b: float32 [2, 256, 2048], P(None, None, ('dp', 'ctx'))
The draws below stay inside these ranges and needn't reach their ends.
All inputs are finite; a program needn't handle non-finite values.
Results may differ from the reference program's by a relative error of at most 0.015.
Values may be sent and summed in bfloat16 or wider, within the bound.
No kernel may reach another device: no remote copies, remote signals or barrier semaphores. Data moves between devices by JAX's collectives and lax.ppermute only.
A program may use at most 320 MiB of HBM per device.

```python
import jax
import jax.numpy as jnp
from jax import lax

MODEL_WIDTH = 2048
QUERY_HEADS = 8
HEAD_WIDTH = 256
HIDDEN_UNITS = 16384
RANK_WIDTH = 256
LOOP_COUNT = 2
QUERY_FEATURES = 2048
GROUP = 256
TOKENS = 1024
N_DP = 4


def with_ends(entries, key, smallest, top_value):
    longest = entries.shape.index(max(entries.shape))
    spots = []
    for shift in (0, 1):
        where = [jax.random.randint(jax.random.fold_in(key, axis), (), 0, length) for axis, length in enumerate(entries.shape)]
        where[longest] = (where[longest] + shift) % entries.shape[longest]
        spots.append(tuple(where))
    return entries.at[spots[0]].set(smallest).at[spots[1]].set(top_value)


def raised(values, stream_key, source, target, parts, factor):
    def block_of(position):
        return (jnp.arange(values.shape[position]) // (values.shape[position] // parts)).reshape((-1,) + (1,) * (values.ndim - 1 - position))

    one_side = jax.random.permutation(stream_key, parts)[block_of(target)]
    second = (block_of(target) + parts // 2) % parts
    return jnp.where((block_of(source) == one_side) | (block_of(source) == second), factor * values, values)


def block_scale(stream_key, dims, shards, smallest, high):
    gain = 1.0
    for axis_at, blocks in shards:
        draws = jax.random.uniform(jax.random.fold_in(jax.random.fold_in(stream_key, 6), axis_at), (blocks,), jnp.float32, smallest / len(shards), high / len(shards))
        gain = gain * jnp.repeat(jnp.exp(draws), dims[axis_at] // blocks).reshape((-1,) + (1,) * (len(dims) - 1 - axis_at))
    return gain


def normal_values(key, shape, width, reach, pieces=(), held_as=jnp.bfloat16):
    level = block_scale(key, shape, pieces, -0.22, 0.18) if pieces else 1.0
    entries = jax.random.normal(key, shape, jnp.float32) * width * level
    return jnp.minimum(jnp.maximum(entries, -reach), reach).astype(held_as)


def bell_draw_with(own_key, extent, spread, limit, cuts, heavy, kind=jnp.bfloat16):
    result = spread * jax.random.normal(own_key, extent, jnp.float32)
    if cuts:
        result = result * block_scale(own_key, extent, cuts, -0.22, 0.18)
    return jnp.clip(raised(result, jax.random.fold_in(own_key, 3), *heavy), -limit, limit).astype(kind)


def setup_inputs(seed: int = 0) -> dict:
    splits = jax.random.split(jax.random.key(seed), 17)
    tokens = normal_values(splits[0], (TOKENS, MODEL_WIDTH), 1.0, 6.0, ((0, 8),))
    cotangent = bell_draw_with(splits[1], (TOKENS, MODEL_WIDTH), 1.0, 6.0, ((0, 8),), (0, 1, 8, 2.0))
    sequence_loops = with_ends(jax.random.randint(splits[2], (N_DP,), 0, LOOP_COUNT), jax.random.fold_in(splits[2], 1), 0, LOOP_COUNT - 1).astype(jnp.int32)
    attention_gain = jnp.clip(1.0 + 0.18 * jax.random.normal(splits[3], (MODEL_WIDTH,), jnp.float32), 0.099609375, 1.8984375).astype(jnp.bfloat16)
    query_weight = normal_values(splits[4], (MODEL_WIDTH, QUERY_FEATURES), MODEL_WIDTH ** -0.5, 0.125, ((0, 8), (1, 4)))
    key_weight = normal_values(splits[5], (MODEL_WIDTH, HEAD_WIDTH), MODEL_WIDTH ** -0.5, 0.125, ((0, 8),))
    value_weight = normal_values(splits[6], (MODEL_WIDTH, HEAD_WIDTH), MODEL_WIDTH ** -0.5, 0.125, ((0, 8),))
    attention_output_weight = normal_values(splits[7], (QUERY_FEATURES, MODEL_WIDTH), (max(QUERY_HEADS * HEAD_WIDTH // 256, 1)) ** -0.5, 2.0, ((0, 4), (1, 8)))
    lowrank_output_first = normal_values(splits[8], (LOOP_COUNT, QUERY_FEATURES, RANK_WIDTH), (max(QUERY_HEADS * HEAD_WIDTH // 128, 1)) ** -0.5, 1.5, ((1, 32),))
    lowrank_output_second = normal_values(splits[9], (LOOP_COUNT, RANK_WIDTH, MODEL_WIDTH), RANK_WIDTH ** -0.5, 0.375, ((2, 8),))
    feedforward_gain = jnp.clip(1.0 + 0.18 * jax.random.normal(splits[10], (MODEL_WIDTH,), jnp.float32), 0.099609375, 1.8984375).astype(jnp.bfloat16)
    gate_weight = normal_values(splits[11], (MODEL_WIDTH, HIDDEN_UNITS), MODEL_WIDTH ** -0.5, 0.125, ((0, 8), (1, 4)))
    up_weight = normal_values(splits[12], (MODEL_WIDTH, HIDDEN_UNITS), MODEL_WIDTH ** -0.5, 0.125, ((0, 8), (1, 4)))
    down_weight = normal_values(splits[13], (HIDDEN_UNITS, MODEL_WIDTH), HIDDEN_UNITS ** -0.5, 0.046875, ((0, 4), (1, 8)))
    lowrank_down_first = normal_values(splits[14], (LOOP_COUNT, HIDDEN_UNITS, RANK_WIDTH), HIDDEN_UNITS ** -0.5, 0.046875, ((1, 32),))
    lowrank_down_second = normal_values(splits[15], (LOOP_COUNT, RANK_WIDTH, MODEL_WIDTH), RANK_WIDTH ** -0.5, 0.375, ((2, 8),))
    return dict(tokens=tokens, cotangent=cotangent, sequence_loops=sequence_loops, attention_gain=attention_gain, query_weight=query_weight, key_weight=key_weight, value_weight=value_weight, attention_output_weight=attention_output_weight, lowrank_output_first=lowrank_output_first, lowrank_output_second=lowrank_output_second, feedforward_gain=feedforward_gain, gate_weight=gate_weight, up_weight=up_weight, down_weight=down_weight, lowrank_down_first=lowrank_down_first, lowrank_down_second=lowrank_down_second)


@jax.custom_vjp
def low(v):
    return lax.optimization_barrier(v.astype(jnp.bfloat16)).astype(jnp.float32)

@jax.custom_vjp
def lowrank_backward(v):
    return v

def low_keep(v):
    return (low(v), None)

def low_pass(kept, grad):
    return (grad,)

def back_keep(v):
    return (v, None)

def back_low(kept, grad):
    return (low(grad),)
low.defvjp(low_keep, low_pass)
lowrank_backward.defvjp(back_keep, back_low)

def both_directions(value):
    return low(lowrank_backward(value))

def highest_precision(spec, left, right):
    return jnp.einsum(spec, left, right, precision=lax.Precision.HIGHEST)

def rms_apply(values, gain_vec):
    inverse = lax.rsqrt(lax.optimization_barrier(jnp.mean(values * values, axis=-1, keepdims=True)) + 1e-06)
    return values * inverse * gain_vec

def layout(loop_id, group_rows):
    positions = jnp.arange(group_rows, dtype=jnp.int32)
    loop_row = (jnp.arange(LOOP_COUNT, dtype=jnp.int32) == loop_id).astype(jnp.float32)
    select = jnp.zeros((group_rows, LOOP_COUNT), jnp.float32) + loop_row[None, :]
    return (positions, select)

def tables(offset):
    half_width = HEAD_WIDTH // 2
    frequency = 10000.0 ** (-(jnp.arange(half_width, dtype=jnp.float32) * 2.0 / HEAD_WIDTH))
    angles = offset.astype(jnp.float32)[:, None] * frequency[None, :]
    return (jnp.cos(angles), jnp.sin(angles))

def rotate(values, cosine, sine):
    half_width = values.shape[-1] // 2
    first_half = values[..., :half_width]
    second_half = values[..., half_width:]
    return jnp.concatenate([first_half * cosine - second_half * sine, second_half * cosine + first_half * sine], axis=-1)

def group_forward(weight_bundle, inputs):
    gain_one, query_w, key_w, value_w, output_weight, output_first, output_second, gain_two, gate_w, up_w, down_w, down_a, down_b = weight_bundle
    group_in, loop_id = inputs
    positions, select = layout(loop_id, GROUP)
    cosine, sine = tables(positions)
    selected_transposed = select.T[:, :, None]
    normed = low(rms_apply(group_in, gain_one))
    queries = lowrank_backward(highest_precision('td,dc->tc', normed, query_w))
    keys_raw = lowrank_backward(highest_precision('td,dc->tc', normed, key_w))
    values = both_directions(highest_precision('td,dc->tc', normed, value_w))
    query_rot = low(rotate(queries.reshape(GROUP, QUERY_HEADS, HEAD_WIDTH), cosine[:, None, :], sine[:, None, :]))
    key_rot = low(rotate(keys_raw, cosine, sine))
    scores = lowrank_backward(highest_precision('qhd,kd->hqk', query_rot, key_rot) * HEAD_WIDTH ** (-0.5))
    allowed = positions[None, :] <= positions[:, None]
    scores = jnp.where(allowed[None], scores, -1e+30)
    soft_weights = jax.nn.softmax(scores, axis=-1)
    heads_output = both_directions(highest_precision('hqk,kd->qhd', low(soft_weights), values).reshape(GROUP, QUERY_HEADS * HEAD_WIDTH))
    lowrank_middle = both_directions(lax.optimization_barrier(jnp.sum(highest_precision('wq,dqs->dws', heads_output, output_first) * selected_transposed, axis=0)))
    attention_total = lowrank_backward(highest_precision('fo,ow->fw', heads_output, output_weight) + highest_precision('ivn,inj->vj', lowrank_middle[None] * selected_transposed, output_second))
    resid = group_in + attention_total
    normed_two = low(rms_apply(resid, gain_two))
    gate_proj = lowrank_backward(highest_precision('td,df->tf', normed_two, gate_w))
    up_proj = lowrank_backward(highest_precision('td,df->tf', normed_two, up_w))
    inner_act = low(jax.nn.gelu(gate_proj, approximate=True) * up_proj)
    down_mid = both_directions(lax.optimization_barrier(jnp.sum(highest_precision('tf,lfr->ltr', inner_act, down_a) * selected_transposed, axis=0)))
    mlp_total = lowrank_backward(highest_precision('tf,fd->td', inner_act, down_w) + highest_precision('ivn,inj->vj', down_mid[None] * selected_transposed, down_b))
    return resid + mlp_total

def reference(tokens, cotangent, sequence_loops, attention_gain, query_weight, key_weight, value_weight, attention_output_weight, lowrank_output_first, lowrank_output_second, feedforward_gain, gate_weight, up_weight, down_weight, lowrank_down_first, lowrank_down_second):
    weight_bundle = tuple((entry_value.astype(jnp.float32) for entry_value in (attention_gain, query_weight, key_weight, value_weight, attention_output_weight, lowrank_output_first, lowrank_output_second, feedforward_gain, gate_weight, up_weight, down_weight, lowrank_down_first, lowrank_down_second)))
    grouped = tokens.astype(jnp.float32).reshape(N_DP, GROUP, MODEL_WIDTH)
    stepper = jax.checkpoint(group_forward)

    def forward(group_inputs, weight_set):

        def scan_body(carried, inputs):
            return (carried, stepper(weight_set, inputs))
        _, results = lax.scan(scan_body, jnp.zeros((), jnp.float32), (group_inputs, sequence_loops))
        return results
    results, pullback = jax.vjp(forward, grouped, weight_bundle)
    input_grads, weight_grads = pullback(cotangent.astype(jnp.float32).reshape(N_DP, GROUP, MODEL_WIDTH))
    out = results.reshape(TOKENS, MODEL_WIDTH).astype(jnp.bfloat16)
    input_grad = input_grads.reshape(TOKENS, MODEL_WIDTH).astype(jnp.bfloat16)
    return (out, input_grad, weight_grads[0], weight_grads[1], weight_grads[2], weight_grads[3], weight_grads[4], weight_grads[5], weight_grads[6], weight_grads[7], weight_grads[8], weight_grads[9], weight_grads[10], weight_grads[11], weight_grads[12])
```

```python
import jax
import jax.numpy as jnp
from jax import lax
from jax.experimental import pallas as pl
from jax.experimental.pallas import tpu as pltpu
from jax.sharding import PartitionSpec as P


HEAD_WIDTH = 256
F32 = jnp.float32
BF16 = jnp.bfloat16


def dot(left, right, dims):
    return lax.dot_general(left, right, (dims, ((), ())), preferred_element_type=F32)


def mm(left, right):
    return dot(left, right, ((1,), (0,)))


def mm_nt(left, right):
    return dot(left, right, ((1,), (1,)))


def mm_tn(left, right):
    return dot(left, right, ((0,), (0,)))


def after(value, *tokens):
    return lax.optimization_barrier((value, *tokens))[0]


def cat(values, axis=0):
    return jnp.concatenate(values, axis=axis) if len(values) > 1 else values[0]


def rotate(values, cosine, sine):
    half = HEAD_WIDTH // 2
    first, second = values[..., :half], values[..., half:]
    return jnp.concatenate([first * cosine - second * sine, second * cosine + first * sine], axis=-1)


def rms_stats(values):
    inverse = lax.rsqrt(jnp.mean(values * values, axis=-1, keepdims=True) + 1e-06)
    return values * inverse, inverse


def rms_back(grads, unit_rows, inverse, gain):
    scaled = grads * gain
    return inverse * (scaled - unit_rows * jnp.mean(scaled * unit_rows, axis=-1, keepdims=True))


def shuffle(scalars, ins, outs, moves):
    count = len(ins)

    def place_of(spec, step, ref):
        return pl.multiple_of(spec(ref), step) if callable(spec) else spec

    def kernel(scalar_ref, *refs):
        for i, r, nr, c, ncol, o, ro, co, mask in moves:
            source = refs[count - i - 1] if i < 0 else refs[i]
            target = refs[count + o]
            row, col = place_of(r, nr, scalar_ref), place_of(c, ncol, scalar_ref)
            row_out, col_out = place_of(ro, nr, scalar_ref), place_of(co, ncol, scalar_ref)
            keep = None if mask is None else mask(scalar_ref)
            chunk = nr
            for size in (64, 32, 16):
                if nr % size == 0 and nr > size:
                    chunk = size
                    break

            def copy(step, row=row, col=col, row_out=row_out, col_out=col_out, keep=keep,
                     source=source, target=target, chunk=chunk, ncol=ncol):
                base = step * chunk
                if chunk % 16 == 0 and not isinstance(base, int):
                    base = pl.multiple_of(base, chunk)
                value = source[pl.ds(row + base, chunk), pl.ds(col, ncol)].astype(target.dtype)
                if keep is not None:
                    value = jnp.where(keep, value, jnp.zeros_like(value))
                target[pl.ds(row_out + base, chunk), pl.ds(col_out, ncol)] = value

            if chunk == nr:
                copy(0)
            else:
                pl.loop(0, nr // chunk)(copy)

    touched = sum(v.size * v.dtype.itemsize for v in list(ins)) + sum(
        o.size * o.dtype.itemsize for o in outs
    )
    return pl.pallas_call(
        kernel,
        out_shape=tuple(outs),
        in_specs=[pl.BlockSpec(memory_space=pltpu.SMEM)]
        + [pl.BlockSpec(memory_space=pltpu.VMEM)] * count,
        out_specs=tuple(pl.BlockSpec(memory_space=pltpu.VMEM) for _ in outs),
        cost_estimate=pl.CostEstimate(flops=0, bytes_accessed=touched, transcendentals=0),
    )(scalars, *ins)


def body(
    tokens,
    cotangent,
    sequence_loops,
    attention_gain,
    query_weight,
    key_weight,
    value_weight,
    attention_output_weight,
    lowrank_output_first,
    lowrank_output_second,
    feedforward_gain,
    gate_weight,
    up_weight,
    down_weight,
    lowrank_down_first,
    lowrank_down_second,
):
    nt, nd, nc = (lax.axis_size(name) for name in ("tensor", "dp", "ctx"))
    assert nc == 2
    ti, di, ci = (lax.axis_index(name) for name in ("tensor", "dp", "ctx"))
    rows, width = tokens.shape
    seq = rows * nc
    sub = rows // nt
    total = seq * nd
    loops, rank = lowrank_output_second.shape[:2]
    own_cols = width // (nd * nc)
    hidden = gate_weight.shape[1]
    fb = hidden // (nd * nc)
    head_cols = query_weight.shape[1]
    split = head_cols // HEAD_WIDTH >= nc
    qf = head_cols // nc if split else head_cols
    nh = qf // HEAD_WIDTH
    first_core = ci == 0
    spots = [(s, k) for k in range(nc) for s in range(nd)]

    def swap(value):
        return lax.ppermute(value, "ctx", [(i, i ^ 1) for i in range(nc)])

    def dperm(value, s):
        return lax.ppermute(value, "dp", [(i, i ^ s) for i in range(nd)]) if s else value

    def tperm(value, s):
        return lax.ppermute(value, "tensor", [(i, i ^ s) for i in range(nt)])

    def send(value, s, k):
        if s == 0:
            return swap(value) if k else value
        if k == 0:
            return dperm(value, s)
        pairs = [(i, i ^ (s * nc + k)) for i in range(nd * nc)]
        return lax.ppermute(value, ("dp", "ctx"), pairs)

    def pick(zero, one):
        return jnp.where(first_core, zero, one)

    def mine_of(value, axis):
        zero, one = jnp.split(value, 2, axis=axis)
        return pick(zero, one)

    def other_of(value, axis):
        zero, one = jnp.split(value, 2, axis=axis)
        return pick(one, zero)

    def pair(mine, other, axis):
        return pick(
            jnp.concatenate([mine, other], axis=axis), jnp.concatenate([other, mine], axis=axis)
        )

    def spread(pieces):
        got = [list(pieces)]
        if nd == 4:
            got.append([dperm(v, 1) for v in pieces])
            got.append([dperm(v, 2) for v in pieces])
            if len(pieces) == 1:
                half = pieces[0].shape[0] // 2
                got.append([dperm(got[1][0][:half], 2), dperm(got[2][0][half:], 1)])
            else:
                last = []
                for i in range(len(pieces)):
                    last.append(dperm(got[1][i], 2) if i % 2 == 0 else dperm(got[2][i], 1))
                got.append(last)
        else:
            for s in range(1, nd):
                got.append([dperm(v, s) for v in pieces])
        return got

    def spread_both(pieces):
        own = spread(pieces)
        return [own, [[swap(v) for v in group] for group in own]]

    def flat(groups):
        return [v for group in groups for v in group]

    def gather_t(value):
        return cat([value] + [tperm(value, z) for z in range(1, nt)])

    def reduce_t(value):
        step = value.shape[0] // nt
        own = value[:step]
        for z in range(1, nt):
            own = own + tperm(value[z * step : (z + 1) * step].astype(BF16), z).astype(F32)
        return own

    def reduce_c(own, other_low):
        return own + swap(other_low).astype(F32)

    def reduce_d(chip):
        got = []
        for s in range(1, nd):
            got.append(dperm(chip[s * rows : (s + 1) * rows].astype(BF16), s))
        return chip[:rows], got

    def total_of(own, got):
        for value in got:
            own = own + value.astype(F32)
        return own

    scalars = jnp.stack([ti, di, ci]).astype(jnp.int32)

    def block_of(s, k, size):
        return lambda ref: ((ref[1] ^ s) * nc + (ref[2] ^ k)) * size

    def masked(value, row_loops):
        return jnp.concatenate(
            [jnp.where(row_loops == l, value, jnp.zeros_like(value)) for l in range(loops)], axis=1
        )

    if split:
        q_zero, q_one = query_weight[:, :qf], query_weight[:, qf:]
    else:
        q_zero = q_one = query_weight
    for_zero = jnp.concatenate([q_zero, key_weight], axis=1)
    for_one = jnp.concatenate([q_one, value_weight], axis=1)
    w_cols = qf + HEAD_WIDTH
    gain_rows = jnp.concatenate([attention_gain, feedforward_gain])
    gain_rows = jnp.pad(gain_rows, (0, 15 * w_cols - gain_rows.shape[0])).reshape(15, w_cols)
    loop_row = jnp.broadcast_to(sequence_loops.astype(BF16)[:, None], (1, w_cols))
    gain_rows = jnp.concatenate([gain_rows, loop_row], axis=0)
    one_mine = jnp.concatenate([pick(for_zero, for_one), gain_rows], axis=0)
    one_got = swap(jnp.concatenate([pick(for_one, for_zero), gain_rows], axis=0))
    one_pieces = spread([one_mine, one_got])

    def z_block(z):
        return lambda ref: (ref[0] ^ z) * sub

    tok_rel, cot_rel = shuffle(
        scalars,
        [tokens, after(cotangent, one_got)],
        [jax.ShapeDtypeStruct(tokens.shape, BF16)] * 2,
        [
            (i, z_block(z), sub, 0, width, i, z * sub, 0, None)
            for i in range(2)
            for z in range(nt)
        ],
    )
    tok_seq = jnp.concatenate([tok_rel, swap(tok_rel)], axis=0)
    cot_t = cat([dperm(cot_rel[:sub], s) for s in range(nd)])
    cot_own = [cot_t] + [tperm(cot_t, z) for z in range(1, nt)]

    gu_out = shuffle(
        scalars,
        [after(gate_weight, one_got), up_weight],
        [jax.ShapeDtypeStruct((own_cols, 2 * fb), BF16)] * (nd * nc),
        [
            (g, 0, own_cols, block_of(s, k, fb), fb, j, 0, g * fb, None)
            for j, (s, k) in enumerate(spots)
            for g in range(2)
        ],
    )

    moves = []
    for s in range(nd):
        for k in range(nc):
            i = s * nc + k
            moves.append((i, 0, own_cols, 0, w_cols, 0, block_of(s, k, own_cols), 0, None))
            for g in range(2):
                at = g * own_cols
                moves.append(
                    (i, own_cols + at // w_cols, 1, at % w_cols, own_cols, 1, g,
                     block_of(s, k, own_cols), None)
                )
        moves.append((s * nc, own_cols + 15, 1, 0, 128, 1, 2, s * 128, None))
    w_one, gains = shuffle(
        scalars,
        flat(one_pieces),
        [
            jax.ShapeDtypeStruct((width, w_cols), BF16),
            jax.ShapeDtypeStruct((8, width), F32),
        ],
        moves,
    )
    gain_one, gain_two = gains[0:1], gains[1:2]
    loop_rel = gains[2, : nd * 128].reshape(nd, 128)[:, 0].astype(jnp.int32)
    scalars = jnp.concatenate([scalars, loop_rel])
    row_loop = jnp.broadcast_to(loop_rel[None, :, None], (nc, nd, rows)).reshape(total, 1)
    seq_loop = jnp.broadcast_to(loop_rel[:, None], (nd, seq)).reshape(total, 1)

    if split:
        o_mine = mine_of(attention_output_weight, 0)
        o_other = other_of(attention_output_weight, 0)
    else:
        o_mine = o_other = attention_output_weight
    o_rows = o_mine.shape[0]
    a_rows = lowrank_output_first.shape[1]
    groups = rank // own_cols
    o_both = jnp.concatenate([o_mine, swap(o_other)], axis=0)
    o_both = after(o_both, one_pieces[-1][-1])
    o_all = [o_both] + [dperm(o_both, s) for s in range(1, nd)]
    low_out = shuffle(
        scalars,
        [
            lowrank_output_second.reshape(loops * rank, own_cols),
            lowrank_down_second.reshape(loops * rank, own_cols),
            lowrank_output_first.reshape(loops * a_rows, rank),
        ],
        [jax.ShapeDtypeStruct((2 * rank + groups * a_rows, own_cols), BF16)] * nd,
        [
            (i, lambda ref, s=s: ref[3 + s] * rank, rank, 0, own_cols, s, i * rank, 0, None)
            for s in range(nd)
            for i in range(2)
        ]
        + [
            (2, lambda ref, s=s: ref[3 + s] * a_rows, a_rows, g * own_cols, own_cols, s,
             2 * rank + g * a_rows, 0, None)
            for s in range(nd)
            for g in range(groups)
        ],
    )
    low_own = [dperm(v, s) for s, v in enumerate(low_out)]
    low_all = low_own + [swap(v) for v in low_own]
    moves = []
    for s in range(nd):
        for k in range(nc):
            col = block_of(s, k, own_cols)
            moves.append((s, k * o_rows, o_rows, 0, own_cols, 0, 0, col, None))
            i = nd + k * nd + s
            moves.append((i, 0, rank, 0, own_cols, 1, 0, col, None))
            moves.append((i, rank, rank, 0, own_cols, 2, 0, col, None))
            for g in range(groups):
                moves.append(
                    (i, 2 * rank + g * a_rows, a_rows, 0, own_cols, 3,
                     block_of(s, k, a_rows), g * own_cols, None)
                )
    head_row = (lambda ref: ref[2] * qf) if split else 0
    moves.append((-4, head_row, qf, 0, rank, 0, 0, width, None))
    wo_cat, out_second, down_second, _ = shuffle(
        scalars,
        o_all + low_all,
        [
            jax.ShapeDtypeStruct((o_rows, width + rank), BF16),
            jax.ShapeDtypeStruct((rank, width), BF16),
            jax.ShapeDtypeStruct((rank, width), BF16),
            jax.ShapeDtypeStruct((head_cols, rank), BF16),
        ],
        moves,
    )

    gu_got = [
        send(after(v, o_all[-1], low_own[-1]) if s else v, s, k)
        for v, (s, k) in zip(gu_out, spots)
    ]

    own_rows = jnp.concatenate(
        [(ti ^ z) * sub + jnp.arange(sub, dtype=jnp.int32) for z in range(nt)]
    )
    positions = jnp.concatenate([ci * rows + own_rows, (1 - ci) * rows + own_rows])
    half_width = HEAD_WIDTH // 2
    frequency = 10000.0 ** (-(jnp.arange(half_width, dtype=F32) * 2.0 / HEAD_WIDTH))
    angles = positions.astype(F32)[:, None] * frequency[None, :]
    cosine, sine = jnp.cos(angles), jnp.sin(angles)
    allowed = positions[None, :] <= positions[:, None]
    score_scale = HEAD_WIDTH ** (-0.5)
    unit_one, inverse_one = rms_stats(tok_seq.astype(F32))
    normed_one = (unit_one * gain_one).astype(BF16)
    projected = mm(normed_one, w_one)
    kv_raw = projected[:, qf:]
    kv_own = pick(rotate(kv_raw, cosine, sine), kv_raw).astype(BF16)
    kv_other = swap_rows = swap(kv_own)
    kv_other = jnp.concatenate([swap_rows[rows:], swap_rows[:rows]], axis=0)
    key_rot, values = pick(kv_own, kv_other), pick(kv_other, kv_own)
    heads, softs, query_rots = [], [], []
    for h in range(nh):
        query_rot = rotate(
            projected[:, h * HEAD_WIDTH : (h + 1) * HEAD_WIDTH], cosine, sine
        ).astype(BF16)
        scores = jnp.where(allowed, mm_nt(query_rot, key_rot) * score_scale, -1e30)
        exp_terms = jnp.exp(scores - jnp.max(scores, axis=-1, keepdims=True))
        soft = exp_terms / jnp.sum(exp_terms, axis=-1, keepdims=True)
        heads.append(mm(soft.astype(BF16), values).astype(BF16))
        softs.append(soft)
        query_rots.append(query_rot)
    heads_out = cat(heads, 1)

    def for_rows(value):
        if split:
            return value
        return jnp.concatenate([value[:rows], jnp.zeros_like(value[rows:])], axis=0)

    summed = for_rows(heads_out)
    part_other = mm(summed[rows:], wo_cat).astype(BF16)
    part_own = mm(summed[:rows], wo_cat)
    attention_sum = reduce_t(part_own + swap(part_other).astype(F32))
    lora_mid = attention_sum[:, width:].astype(BF16)
    own_tokens = tok_rel[:sub].astype(F32)
    resid = own_tokens + attention_sum[:, :width] + mm(lora_mid, out_second)
    unit_two, inverse_two = rms_stats(resid)
    normed_two = (unit_two * gain_two).astype(BF16)
    two_t = gather_t(jnp.concatenate([normed_two, lora_mid], axis=1))
    two_pieces = spread_both([two_t])
    ins, moves = [], []
    for k in range(nc):
        for s in range(nd):
            at = 0
            for piece in two_pieces[k][s]:
                height = piece.shape[0]
                moves.append(
                    (len(ins), 0, height, 0, width, 0, (k * nd + s) * rows + at, 0, None)
                )
                moves.append(
                    (len(ins), 0, height, width, rank, 1, (s * nc + k) * rows + at, 0, None)
                )
                ins.append(piece)
                at += height
    normed_all, lora_mid_all = shuffle(
        scalars,
        ins,
        [
            jax.ShapeDtypeStruct((total, width), BF16),
            jax.ShapeDtypeStruct((total, rank), BF16),
        ],
        moves,
    )

    gu_got = [after(v, two_t) for v in gu_got]
    (gu_w,) = shuffle(
        scalars,
        gu_got,
        [jax.ShapeDtypeStruct((width, 2 * fb), BF16)],
        [
            (j, 0, own_cols, 0, 2 * fb, 0, block_of(s, k, own_cols), 0, None)
            for j, (s, k) in enumerate(spots)
        ],
    )
    down_out = shuffle(
        scalars,
        [after(down_weight, one_got)],
        [jax.ShapeDtypeStruct((fb, own_cols), BF16)] * (nd * nc),
        [
            (0, block_of(s, k, fb), fb, 0, own_cols, j, 0, 0, None)
            for j, (s, k) in enumerate(spots)
        ],
    )
    down_got = [
        send(after(v, *two_pieces[0][-1]) if s else v, s, k)
        for v, (s, k) in zip(down_out, spots)
    ]
    cat_cols = width + loops * rank
    (down_cat,) = shuffle(
        scalars,
        down_got + [lowrank_down_first[l] for l in range(loops)],
        [jax.ShapeDtypeStruct((fb, cat_cols), BF16)],
        [
            (j, 0, fb, 0, own_cols, 0, 0, block_of(s, k, own_cols), None)
            for j, (s, k) in enumerate(spots)
        ]
        + [
            (nd * nc + l, 0, fb, 0, rank, 0, 0, width + l * rank, None) for l in range(loops)
        ],
    )

    mid_grad_own = mm_nt(after(cot_rel, two_t), down_second).astype(BF16)
    mg_own = cat([dperm(mid_grad_own, s) for s in range(nd)])
    mg_pieces = [mg_own, swap(mg_own)]
    cot_all = cot_own + [swap(v) for v in cot_own]
    moves = []
    for k in range(nc):
        for s in range(nd):
            for z in range(nt):
                moves.append(
                    (k * nt + z, s * sub, sub, 0, width, 0, (k * nd + s) * rows + z * sub, 0, None)
                )
            for l in range(loops):
                moves.append(
                    (nc * nt + k, s * rows, rows, 0, rank, 0, (k * nd + s) * rows,
                     width + l * rank, lambda ref, s=s, l=l: ref[3 + s] == l)
                )
    (cot_cat,) = shuffle(
        scalars, cot_all + mg_pieces, [jax.ShapeDtypeStruct((total, cat_cols), BF16)], moves
    )

    gate_up = mm(normed_all, gu_w)
    gate, up = gate_up[:, :fb], gate_up[:, fb:]
    root = (2.0 / jnp.pi) ** 0.5
    inside = jnp.tanh(root * (gate + 0.044715 * gate * gate * gate))
    gelu = 0.5 * gate * (1.0 + inside)
    slope = 0.5 * (1.0 + inside) + 0.5 * gate * (1.0 - inside * inside) * root * (
        1.0 + 3.0 * 0.044715 * gate * gate
    )
    inner = (gelu * up).astype(BF16)
    inner_grad = mm_nt(cot_cat, down_cat)
    gu_grad = jnp.concatenate(
        [(inner_grad * up * slope).astype(BF16), (inner_grad * gelu).astype(BF16)], axis=1
    )
    half_total = total // 2
    two_other = mm_nt(gu_grad[half_total:], gu_w).astype(BF16)
    two_own = mm_nt(gu_grad[:half_total], gu_w)
    two_chip, two_got = reduce_d(reduce_c(two_own, two_other))
    normed_two_grad = reduce_t(total_of(two_chip, two_got))
    inner, gu_grad = after((inner, gu_grad), two_own)

    def mlp_rows(lo, hi):
        product = mm(inner[lo:hi], down_cat)
        middle = product[:, width : width + rank]
        for l in range(1, loops):
            middle = jnp.where(
                row_loop[lo:hi] == l,
                product[:, width + l * rank : width + (l + 1) * rank],
                middle,
            )
        return jnp.concatenate([product[:, :width], middle], axis=1)

    mlp_other = mlp_rows(half_total, total).astype(BF16)
    mlp_own = mlp_rows(0, half_total)
    mlp_chip = reduce_c(mlp_own, mlp_other)
    mlp_chip, mlp_got = reduce_d(after(mlp_chip, *two_got))

    gu_grad_w = mm_tn(normed_all, gu_grad).astype(BF16)
    gu_grid = gu_grad_w.reshape(nd * nc, own_cols, 2 * fb)
    gu_back = []
    for s, k in spots:
        value = lax.dynamic_index_in_dim(gu_grid, (di ^ s) * nc + (ci ^ k), 0, keepdims=False)
        gu_back.append(send(after(value, *mlp_got) if s else value, s, k))
    grad_gate, grad_up = shuffle(
        scalars,
        gu_back,
        [jax.ShapeDtypeStruct((own_cols, hidden), F32)] * 2,
        [
            (j, 0, own_cols, g * fb, fb, g, 0, block_of(s, k, fb), None)
            for j, (s, k) in enumerate(spots)
            for g in range(2)
        ],
    )
    down_grad_cat = mm_tn(inner, cot_cat)
    down_deal = shuffle(
        scalars,
        [down_grad_cat],
        [jax.ShapeDtypeStruct((fb, own_cols), BF16)] * (nd * nc)
        + [jax.ShapeDtypeStruct((loops * fb, rank), F32)],
        [
            (0, 0, fb, block_of(s, k, own_cols), own_cols, j, 0, 0, None)
            for j, (s, k) in enumerate(spots)
        ]
        + [
            (0, 0, fb, width + l * rank, rank, nd * nc, l * fb, 0, None) for l in range(loops)
        ],
    )
    grad_down_a = down_deal[-1].reshape(loops, fb, rank)
    down_back = [send(after(v, *mlp_got) if s else v, s, k) for v, (s, k) in zip(down_deal, spots)]
    (grad_down,) = shuffle(
        scalars,
        down_back,
        [jax.ShapeDtypeStruct((nd * nc * fb, own_cols), F32)],
        [
            (j, 0, fb, 0, own_cols, 0, block_of(s, k, fb), 0, None)
            for j, (s, k) in enumerate(spots)
        ],
    )
    (cot_block,) = shuffle(
        scalars,
        [cot_cat],
        [jax.ShapeDtypeStruct((total, own_cols), BF16)],
        [(0, 0, total, block_of(0, 0, own_cols), own_cols, 0, 0, 0, None)],
    )
    own_cot = cot_rel[:sub].astype(F32)
    resid_grad = own_cot + rms_back(normed_two_grad, unit_two, inverse_two, gain_two)
    gain_two_part = jnp.sum(normed_two_grad * unit_two, axis=0)
    low_rows = gather_t(resid_grad.astype(BF16))
    resid_low = jnp.concatenate([low_rows, swap(low_rows)], axis=0)
    lora_mid_grad = mm_nt(resid_low, out_second).astype(BF16)
    low_cat = jnp.concatenate([resid_low, lora_mid_grad], axis=1)
    heads_grad = mm_nt(low_cat, wo_cat).astype(BF16)

    query_lows = []
    key_sum = value_sum = 0.0
    for h in range(nh):
        head_grad = heads_grad[:, h * HEAD_WIDTH : (h + 1) * HEAD_WIDTH]
        soft_grad = mm_nt(head_grad, values)
        row_dot = jnp.sum(soft_grad * softs[h], axis=-1, keepdims=True)
        score_grad = (softs[h] * (soft_grad - row_dot)).astype(BF16) * score_scale
        score_grad = score_grad.astype(BF16)
        query_lows.append(rotate(mm(score_grad, key_rot), cosine, -sine).astype(BF16))
        key_sum = key_sum + mm_tn(score_grad, query_rots[h])
        value_sum = value_sum + mm_tn(softs[h].astype(BF16), head_grad)
    query_low = cat(query_lows, 1)
    key_part = rotate(key_sum, cosine, -sine)
    kv_sum = pick(key_part, value_sum)
    if split:
        passed = swap(pick(value_sum, key_part).astype(BF16)).astype(F32)
        kv_sum = kv_sum + jnp.concatenate([passed[rows:], passed[:rows]], axis=0)
    grads_one = jnp.concatenate([for_rows(query_low), kv_sum.astype(BF16)], axis=1)
    one_other = mm_nt(grads_one[rows:], w_one)
    one_own = mm_nt(grads_one[:rows], w_one)
    gain_one_part = jnp.sum(one_own * unit_one[:rows], axis=0) + jnp.sum(
        one_other * unit_one[rows:], axis=0
    )
    normed_one_grad = reduce_t(reduce_c(one_own, one_other.astype(BF16)))
    mlp_sum = total_of(mlp_chip, [after(v, one_own) for v in mlp_got])
    mid_low = mlp_sum[:, width:].astype(BF16)
    mid_all = mlp_sum[:, width:]
    for z in range(1, nt):
        mid_z = tperm(mid_low, z).reshape(nt, sub, rank)
        mid_z = jnp.stack([mid_z[y ^ z] for y in range(nt)]).reshape(rows, rank)
        mid_all = mid_all + mid_z.astype(F32)
    mid_all = mid_all.astype(BF16)
    mlp_own = reduce_t(mlp_sum[:, :width])
    out_own = (resid + mlp_own + mm(mid_all[:sub], down_second)).astype(BF16)
    down_mid_own = cat([dperm(mid_all, s) for s in range(nd)])
    down_mid_all = jnp.concatenate([down_mid_own, swap(down_mid_own)], axis=0)
    grad_down_b = mm_tn(masked(down_mid_all, row_loop), cot_block)
    grad_down_b = grad_down_b.reshape(loops, rank, own_cols)
    input_own = resid_grad + rms_back(
        normed_one_grad, unit_one[:sub], inverse_one[:sub], gain_one
    )

    def rows_home(value):
        pieces = [value] + [tperm(value, z) for z in range(1, nt)]
        (placed,) = shuffle(
            scalars,
            pieces,
            [jax.ShapeDtypeStruct((rows, width), BF16)],
            [(z, 0, sub, 0, width, 0, z_block(z), 0, None) for z in range(nt)],
        )
        return placed

    outputs = rows_home(out_own)
    input_grad = rows_home(input_own.astype(BF16))

    def columns_for(value, extra):
        more = extra.shape[1]
        sent = shuffle(
            scalars,
            [value, extra],
            [jax.ShapeDtypeStruct((seq, own_cols + more), BF16)] * nd,
            [
                (0, 0, seq, block_of(s, 0, own_cols), own_cols, s, 0, 0, None)
                for s in range(nd)
            ]
            + [(1, 0, seq, 0, more, s, 0, own_cols, None) for s in range(nd)],
        )
        got = [dperm(v, s) for s, v in enumerate(sent)]
        return cat([v[:, :own_cols] for v in got]), cat([v[:, own_cols:] for v in got])

    def both_heads(own):
        if not split:
            return own
        other = swap(own)
        other = other.reshape(nd, nc, rows, qf)[:, ::-1].reshape(total, qf)
        return pair(own, other, 1)

    one_cols, heads_own = columns_for(after(normed_one, down_cat), heads_out)
    heads_all = both_heads(heads_own)
    low_cols, mid_grad_all = columns_for(resid_low, lora_mid_grad)
    query_all = both_heads(cat([dperm(query_low, s) for s in range(nd)]))

    step = rows // nt
    kv_blocks = kv_sum.reshape(nc, nt, step, HEAD_WIDTH)
    kv_z = kv_blocks[:, 0]
    for z in range(1, nt):
        kv_z = kv_z + tperm(kv_blocks[:, z].astype(BF16), z).astype(F32)
    kv_z = kv_z.astype(BF16).reshape(nc * step, HEAD_WIDTH)
    gain_pack = jnp.concatenate([gain_one_part, gain_two_part]).astype(BF16)
    gain_pack = gain_pack.reshape(-1, HEAD_WIDTH)
    extra = gain_pack.shape[0]
    kv_t = gather_t(jnp.concatenate([kv_z, gain_pack], axis=0))
    kv_pieces = [kv_t] + [dperm(kv_t, s) for s in range(1, nd)]
    kv_grid = jnp.stack(kv_pieces).reshape(nd, nt, nc * step + extra, HEAD_WIDTH)
    kv_mine = kv_grid[:, :, : nc * step].reshape(nd, nt, nc, step, HEAD_WIDTH)
    kv_mine = kv_mine.transpose(0, 2, 1, 3, 4).reshape(total, HEAD_WIDTH)
    kv_back = swap(kv_mine).reshape(nd, nc, rows, HEAD_WIDTH)[:, ::-1]
    kv_back = kv_back.reshape(total, HEAD_WIDTH)
    key_all, value_all = pick(kv_mine, kv_back), pick(kv_back, kv_mine)
    gain_sum = jnp.sum(kv_grid[:, :, nc * step :].astype(F32), axis=(0, 1))
    gain_sum = gain_sum + swap(gain_sum.astype(BF16)).astype(F32)
    gain_sum = gain_sum.reshape(2, nd * nc, own_cols)
    block = di * nc + ci
    gain_own = lax.dynamic_index_in_dim(gain_sum, block, 1, keepdims=False)

    grad_query = mm_tn(one_cols, query_all)
    grad_key = mm_tn(one_cols, key_all)
    grad_value = mm_tn(one_cols, value_all)
    grad_out = mm_tn(heads_all, low_cols)
    out_a = mm_tn(heads_all, masked(mid_grad_all, seq_loop))
    out_a = lax.dynamic_slice_in_dim(out_a, block * a_rows, a_rows, 0)
    grad_out_a = jnp.stack([out_a[:, l * rank : (l + 1) * rank] for l in range(loops)])
    grad_out_b = mm_tn(masked(lora_mid_all, seq_loop), low_cols).reshape(loops, rank, own_cols)
    return (
        outputs,
        input_grad,
        gain_own[0],
        grad_query,
        grad_key,
        grad_value,
        grad_out,
        grad_out_a,
        grad_out_b,
        gain_own[1],
        grad_gate,
        grad_up,
        grad_down,
        grad_down_a,
        grad_down_b,
    )


def solution(mesh):
    both = ("dp", "ctx")
    every = ("tensor", "dp", "ctx")
    params = (
        P(both),
        P(both, "tensor"),
        P(both, None),
        P(both, None),
        P("tensor", both),
        P(None, every, None),
        P(None, None, both),
        P(both),
        P(both, "tensor"),
        P(both, "tensor"),
        P("tensor", both),
        P(None, every, None),
        P(None, None, both),
    )
    rows = (P(both, None), P(both, None))

    return jax.shard_map(
        body,
        mesh=mesh,
        in_specs=rows + (P("dp"),) + params,
        out_specs=rows + params,
        check_vma=False,
    )
```
